32 devices in a mesh: conv: 2 (over y), ctx: 4 (over x, core), head: 4 (over z).
Axes of the slice: x: 2, y: 2, z: 4, core: 2. Of those that a mesh axis runs over, the one named last changes fastest.
Arguments:
- queries: bfloat16 [512, 64, 128], P(('conv', 'ctx'), 'head'), parts along dimension 0, may hold values from -240 to 240, as said below
- new_keys: bfloat16 [512, 8, 128], P(('conv', 'ctx'), 'head'), parts along dimension 0, may hold values from -8 to 8
- new_values: bfloat16 [512, 8, 128], P(('conv', 'ctx'), 'head'), parts along dimension 0, may hold values from -18 to 18
- cache_keys: bfloat16 [16384, 8, 128], P(('conv', 'ctx'), 'head'), parts along dimension 0, may hold values from -6 to 6
- cache_values: bfloat16 [16384, 8, 128], P(('conv', 'ctx'), 'head'), parts along dimension 0, may hold values from -18 to 18
- cache_len: int32 [2], P('conv'), parts along dimension 0, may hold values from 4097 to 8192
Outputs:
- attended: bfloat16 [512, 64, 128], P(('conv', 'ctx'), 'head'), parts along dimension 0
The draws below stay inside these ranges and needn't reach their ends.
There are 2 independent parts, one for each index of `conv`. The reference program is written for one: setup_inputs(seed, part) draws one part's arguments, and reference() takes and returns one part's arrays. A program takes and returns all parts, laid end to end along the dimension named above; each array names one. Nothing has to cross between parts.
Inputs may be any that keep to these rules, and one draw needn't show every extreme that they name: `queries`: each query row is a row of independent entries times a row scale.
All inputs are finite; a program needn't handle non-finite values.
Results may differ from the reference program's by a relative error of at most 0.01.
Values may be sent and summed in bfloat16 or wider, within the bound.
A program may use at most 64 MiB of HBM per device.

```python
import math
import jax
import jax.numpy as jnp
from jax import lax

HQ = 64
KVH = 8
HD = 128
CACHE_DEV = 2048
TNEW = 256
CACHE = 8192
N_CTX = 4


def draw_queries(key, part):
    first, second = jax.random.split(jax.random.fold_in(key, 17), 2)
    base = jnp.clip(jax.random.normal(first, (TNEW, HQ, HD), jnp.float32), -4.0, 4.0)
    scale = jnp.exp(jax.random.uniform(second, (TNEW, HQ, 1), jnp.float32, jnp.log(1.5), jnp.log(3.2)))
    return (base * scale).astype(jnp.bfloat16)


def block_levels(stream_key, shape, pieces, least, top_value):
    def one(position, shards_of):
        draws = jax.random.uniform(jax.random.fold_in(jax.random.fold_in(stream_key, 6), position), (shards_of,), jnp.float32, least / len(pieces), top_value / len(pieces))
        return jnp.repeat(jnp.exp(draws), shape[position] // shards_of).reshape((-1,) + (1,) * (len(shape) - position - 1))

    gain = one(*pieces[0])
    for cut in pieces[1:]:
        gain = gain * one(*cut)
    return gain


def scatter_about(own_key, shape, scale, most, pieces=(), kind=jnp.bfloat16):
    values = scale * jax.random.normal(own_key, shape, jnp.float32)
    if pieces:
        values = values * block_levels(own_key, shape, pieces, -0.22, 0.18)
    return jnp.clip(values, -most, most).astype(kind)


def setup_inputs(seed: int = 0, part: int = 0) -> dict:
    arg_keys = jax.random.split(jax.random.key(seed), 7)
    part_keys = jax.random.split(jax.random.fold_in(arg_keys[6], part), 7)
    return {
        "queries": draw_queries(jax.random.fold_in(jax.random.fold_in(arg_keys[6], part), 71), part),
        "new_keys": scatter_about(part_keys[1], (TNEW, KVH, HD), 1.6, 8.0, ((0, 4), (1, 4))),
        "new_values": scatter_about(part_keys[2], (TNEW, KVH, HD), 3.0, 18.0, ((0, 4), (1, 4))),
        "cache_keys": scatter_about(part_keys[3], (CACHE, KVH, HD), 1.0, 6.0, ((0, 4), (1, 4))),
        "cache_values": scatter_about(part_keys[4], (CACHE, KVH, HD), 3.0, 18.0, ((0, 4), (1, 4))),
        "cache_len": jax.random.randint(part_keys[5], (1,), CACHE // 2 + 1, CACHE + 1).astype(jnp.int32),
    }


def partial_attend(query_rows, keys, values, valid):
    scores = jnp.einsum('tkgd,skd->tkgs', query_rows.astype(jnp.float32), keys.astype(jnp.float32)) * (1.0 / math.sqrt(HD))
    mask = valid[:, None, None, :]
    scores = jnp.where(mask, scores, jnp.float32(-1e+30))
    peak = lax.optimization_barrier(jnp.max(scores, axis=-1))
    expo = jnp.where(mask, jnp.exp(scores - peak[..., None]), jnp.float32(0.0))
    total = lax.optimization_barrier(jnp.sum(expo, axis=-1))
    rounded = lax.optimization_barrier(expo.astype(jnp.bfloat16)).astype(jnp.float32)
    out = jnp.einsum('tkgs,skd->tkgd', rounded, values.astype(jnp.float32))
    return (out, peak, total)

def reference(queries, new_keys, new_values, cache_keys, cache_values, cache_len):
    group = HQ // KVH
    grouped = queries.reshape(TNEW, KVH, group, HD)
    limit = cache_len[0]

    def one_shard(index):
        start = (index * CACHE_DEV).astype(jnp.int32)
        keys = lax.dynamic_slice_in_dim(cache_keys, start, CACHE_DEV, 0)
        values = lax.dynamic_slice_in_dim(cache_values, start, CACHE_DEV, 0)
        slot_ids = start + jnp.arange(CACHE_DEV, dtype=jnp.int32)
        out, peak, total = partial_attend(grouped, keys, values, (slot_ids < limit)[None, :])
        floored = jnp.maximum(total, 1.0)
        norm = lax.optimization_barrier((out / floored[..., None]).astype(jnp.bfloat16)).astype(jnp.float32)
        return (norm, peak + jnp.log(floored))
    norms, lses = lax.map(one_shard, jnp.arange(N_CTX, dtype=jnp.int32))
    token_ids = jnp.arange(TNEW, dtype=jnp.int32)
    causal = token_ids[None, :] <= token_ids[:, None]
    turn_out, turn_max, turn_total = partial_attend(grouped, new_keys, new_values, causal)
    top = jnp.maximum(lax.optimization_barrier(jnp.max(lses, axis=0)), turn_max)
    shard_scale = jnp.exp(lses - top[None])
    turn_scale = jnp.exp(turn_max - top)
    numer = lax.optimization_barrier(jnp.sum(norms * shard_scale[..., None], axis=0)) + turn_out * turn_scale[..., None]
    denom = lax.optimization_barrier(jnp.sum(shard_scale, axis=0)) + turn_total * turn_scale
    result = numer / denom[..., None]
    return result.reshape(TNEW, HQ, HD).astype(jnp.bfloat16)
```

```python
import functools
import math

import jax
import jax.numpy as jnp
from jax import lax
from jax.experimental import pallas as pl
from jax.experimental.pallas import tpu as pltpu
from jax.sharding import PartitionSpec as P

MESH = pl.DeviceIdType.MESH
NEG = -1e30
CHUNK = 256


def column_to_rows(col):
    rows = col.shape[0]
    return [col[i : i + 128].T[0:1, :] for i in range(0, rows, 128)]


def rows_to_column(row):
    return jnp.broadcast_to(row, (128, 128)).T


def kernel(
    chips, nh, group, sub,
    len_ref, q_hbm, nk_ref, nv_ref, k_hbm, v_hbm,
    out_ref,
    k_in, v_in, split, k_s, v_s, dist, q_own, q_part, q_rem, q_rel,
    own_o, own_l, a_o, a_l,
    sp_o, sp_l, sb_o, sb_l, sr_o, sr_l,
    pp_o, pp_l, pb_o, pb_l, pr_o, pr_l,
    loc_sem, send_sem, recv_sem,
):
    tokens, heads, hd = q_hbm.shape
    slots = k_hbm.shape[0] // nh
    rows = tokens * group
    ext = k_s.shape[1] - slots
    me = lax.axis_index("ctx")
    core = lax.rem(me, 2)
    chip = me // 2
    partner = me + 1 - 2 * core
    far = [lax.rem(chip + d, chips) * 2 + core for d in range(1, chips)]
    counter = iter(range(send_sem.shape[0]))

    def remote(src, dst, dev):
        i = next(counter)
        return pltpu.make_async_remote_copy(
            src_ref=src, dst_ref=dst, send_sem=send_sem.at[i], recv_sem=recv_sem.at[i],
            device_id={"ctx": dev}, device_id_type=MESH,
        )

    loads = [
        pltpu.make_async_copy(k_hbm, k_in, loc_sem.at[0]),
        pltpu.make_async_copy(v_hbm, v_in, loc_sem.at[1]),
        pltpu.make_async_copy(q_hbm, q_own, loc_sem.at[2]),
    ]
    for load in loads:
        load.start()

    barrier = pltpu.get_barrier_semaphore()
    for dev in [partner] + far:
        pl.semaphore_signal(barrier, inc=1, device_id={"ctx": dev}, device_id_type=MESH)
    pl.semaphore_wait(barrier, chips)

    send_q_far = [remote(q_hbm, q_rem.at[d], far[d]) for d in range(chips - 1)]
    send_q_part = remote(q_hbm, q_part, partner)
    send_q_rel = [remote(q_rem.at[d], q_rel.at[d], partner) for d in range(chips - 1)]
    send_pp = [
        (remote(sp_o.at[h], pp_o.at[h], partner), remote(sp_l.at[h], pp_l.at[h], partner))
        for h in range(nh)
    ]
    send_pb = [
        [
            (
                remote(sb_o.at[d, h], pb_o.at[d, h], partner),
                remote(sb_l.at[d, h], pb_l.at[d, h], partner),
            )
            for h in range(nh)
        ]
        for d in range(chips - 1)
    ]
    back = [lax.rem(chip + chips - 1 - d, chips) * 2 + core for d in range(chips - 1)]
    send_pr = [
        [
            (
                remote(sr_o.at[d, h], pr_o.at[d, h], back[d]),
                remote(sr_l.at[d, h], pr_l.at[d, h], back[d]),
            )
            for h in range(nh)
        ]
        for d in range(chips - 1)
    ]
    for c in send_q_far:
        c.start()
    send_q_part.start()

    limit = len_ref[0]
    first_slot = me * slots
    filled = first_slot < limit
    loads[0].wait()
    loads[1].wait()
    nk = nk_ref[...].astype(jnp.float32)
    nv = nv_ref[...].astype(jnp.float32)
    k_top = k_in[0:16, :].astype(jnp.float32)
    fill = [jnp.where(filled, k_top[h : h + 1], nk[h : h + 1]) for h in range(nh)]

    def prep(i, _):
        at = pl.multiple_of(i * CHUNK, CHUNK)
        src = pl.ds(pl.multiple_of(i * CHUNK * nh, CHUNK * nh), CHUNK * nh)
        split[0] = k_in[src, :].astype(jnp.float32)
        split[1] = v_in[src, :].astype(jnp.float32)
        ids = first_slot + at + lax.broadcasted_iota(jnp.int32, (CHUNK, hd), 0)
        valid = ids < limit
        ones = jnp.where(valid, 1.0, 0.0).astype(jnp.bfloat16)
        for h in range(nh):
            kh = split[0, pl.ds(h, CHUNK, stride=nh), :]
            vh = split[1, pl.ds(h, CHUNK, stride=nh), :]
            kb = jnp.where(valid, kh, fill[h]).astype(jnp.bfloat16)
            k_s[h, pl.ds(at, CHUNK), 0:hd] = kb
            k_s[h, pl.ds(at, CHUNK), hd : 2 * hd] = kb
            v_s[h, pl.ds(at, CHUNK), 0:hd] = jnp.where(valid, vh, 0.0).astype(jnp.bfloat16)
            v_s[h, pl.ds(at, CHUNK), hd : 2 * hd] = ones
        return 0

    lax.fori_loop(0, slots // CHUNK, prep, 0)
    split[0, 0 : tokens * nh] = nk
    split[1, 0 : tokens * nh] = nv
    for h in range(nh):
        kb = split[0, pl.ds(h, tokens, stride=nh), :].astype(jnp.bfloat16)
        vb = split[1, pl.ds(h, tokens, stride=nh), :].astype(jnp.bfloat16)
        k_s[h, slots : slots + tokens, 0:hd] = kb
        k_s[h, slots : slots + tokens, hd : 2 * hd] = kb
        v_s[h, slots : slots + tokens, 0:hd] = vb
        v_s[h, slots : slots + tokens, hd : 2 * hd] = jnp.ones((tokens, hd), jnp.bfloat16)
        if ext > tokens:
            rest = jnp.zeros((ext - tokens, 2 * hd), jnp.bfloat16)
            k_s[h, slots + tokens :, :] = rest
            v_s[h, slots + tokens :, :] = rest
    row_id = lax.broadcasted_iota(jnp.int32, (rows, ext), 0) // group
    col_id = lax.broadcasted_iota(jnp.int32, (rows, ext), 1)
    dist[...] = jnp.where(col_id < tokens, row_id - col_id, -(2**30))

    scale = math.log2(math.e) / math.sqrt(hd)

    def attend(q_ref, h, block, emit):
        least = (me - block) * tokens
        some = jnp.logical_or(filled, block >= me)
        for r in range(0, rows, sub):
            t = slice(r // group, (r + sub) // group)
            qf = q_ref[t, :, :].astype(jnp.float32)
            qf = qf[:, h * group : (h + 1) * group, :].reshape(sub, hd) * scale
            high = qf.astype(jnp.bfloat16)
            low = (qf - high.astype(jnp.float32)).astype(jnp.bfloat16)
            q2 = jnp.concatenate([high, low], axis=1)
            s = lax.dot_general(
                q2, k_s[h], (((1,), (1,)), ((), ())), preferred_element_type=jnp.float32
            )
            s_new = jnp.where(dist[r : r + sub, :] >= least, s[:, slots:], NEG)
            s_old = s[:, :slots]
            peak = jnp.maximum(
                jnp.max(s_old, axis=1, keepdims=True), jnp.max(s_new, axis=1, keepdims=True)
            )
            p_old = jnp.exp2(s_old - peak).astype(jnp.bfloat16)
            p_new = jnp.exp2(s_new - peak).astype(jnp.bfloat16)
            o = jnp.dot(p_old, v_s[h, :slots, :], preferred_element_type=jnp.float32)
            o = o + jnp.dot(p_new, v_s[h, slots:, :], preferred_element_type=jnp.float32)
            total = jnp.maximum(o[:, hd:], 1.0)
            norm = o[:, :hd] / total
            lse = jnp.where(some, peak + jnp.log2(total), NEG)
            emit(r, norm, lse)

    def keep(o_ref, l_ref):
        def emit(r, norm, lse):
            o_ref[r : r + sub, :] = norm
            l_ref[r : r + sub, :] = lse
        return emit

    def ship(o_ref, l_ref):
        def emit(r, norm, lse):
            o_ref[r : r + sub, :] = norm.astype(jnp.bfloat16)
            for i, row in enumerate(column_to_rows(lse)):
                l_ref[r // 128 + i : r // 128 + i + 1, :] = row
        return emit

    def start(pair):
        pair[0].start()
        pair[1].start()

    def merge(o_ref, l_ref, parts, r):
        outs = [o_ref[r : r + 128, :]]
        lses = [l_ref[r : r + 128, :]]
        for po, pl_ in parts:
            outs.append(po[r : r + 128, :].astype(jnp.float32))
            lses.append(rows_to_column(pl_[r // 128 : r // 128 + 1, :]))
        top = functools.reduce(jnp.maximum, lses)
        weights = [jnp.exp2(l - top) for l in lses]
        den = functools.reduce(jnp.add, weights)
        num = functools.reduce(jnp.add, [w * o for w, o in zip(weights, outs)])
        return num / den, top + jnp.log2(den)

    loads[2].wait()
    send_q_part.wait_recv()
    for h in range(nh):
        attend(q_part, h, partner, ship(sp_o.at[h], sp_l.at[h]))
        start(send_pp[h])
    for h in range(nh - 1):
        attend(q_own, h, me, keep(own_o.at[h], own_l.at[h]))

    for d in range(chips - 1):
        send_q_far[d].wait_recv()
        send_q_rel[d].start()
        a_block = back[d]
        b_block = a_block + 1 - 2 * core

        def join(h, d=d):
            send_pb[d][h][0].wait_recv()
            send_pb[d][h][1].wait_recv()
            for r in range(0, rows, 128):
                norm, lse = merge(
                    a_o.at[h], a_l.at[h], [(pb_o.at[d, h], pb_l.at[d, h])], r
                )
                sr_o[d, h, r : r + 128, :] = norm.astype(jnp.bfloat16)
                sr_l[d, h, r // 128 : r // 128 + 1, :] = column_to_rows(lse)[0]
            start(send_pr[d][h])

        attend(q_rem.at[d], 0, a_block, keep(a_o.at[0], a_l.at[0]))
        send_q_rel[d].wait_recv()
        for h in range(nh):
            attend(q_rel.at[d], h, b_block, ship(sb_o.at[d, h], sb_l.at[d, h]))
            start(send_pb[d][h])
        join(0)
        for h in range(1, nh):
            attend(q_rem.at[d], h, a_block, keep(a_o.at[h], a_l.at[h]))
            join(h)

    attend(q_own, nh - 1, me, keep(own_o.at[nh - 1], own_l.at[nh - 1]))

    for h in range(nh):
        send_pp[h][0].wait_recv()
        send_pp[h][1].wait_recv()
    for d in range(chips - 1):
        for h in range(nh):
            send_pr[d][h][0].wait_recv()
            send_pr[d][h][1].wait_recv()
    for r in range(0, rows, 128):
        pieces = []
        for h in range(nh):
            parts = [(pp_o.at[h], pp_l.at[h])]
            parts += [(pr_o.at[d, h], pr_l.at[d, h]) for d in range(chips - 1)]
            norm, _ = merge(own_o.at[h], own_l.at[h], parts, r)
            pieces.append(norm.reshape(128 // group, group, hd))
        full = jnp.concatenate(pieces, axis=1) if nh > 1 else pieces[0]
        out_ref[r // group : (r + 128) // group, :, :] = full.astype(jnp.bfloat16)

    for c in send_q_far + [send_q_part] + send_q_rel:
        c.wait_send()
    for pair in send_pp + [p for ps in send_pb for p in ps] + [p for ps in send_pr for p in ps]:
        pair[0].wait_send()
        pair[1].wait_send()


def per_device(n_ctx, queries, new_keys, new_values, cache_keys, cache_values, cache_len):
    tokens, heads, hd = queries.shape
    slots, nh, _ = cache_keys.shape
    group = heads // nh
    rows = tokens * group
    chips = n_ctx // 2
    far = chips - 1
    ext = -(-tokens // 128) * 128
    f32, bf16 = jnp.float32, jnp.bfloat16
    lr = rows // 128
    n_copies = far + 1 + far + 2 * nh + 4 * far * nh
    flat = lambda x: x.reshape(x.shape[0] * nh, hd)
    vmem, hbm = pl.BlockSpec(memory_space=pltpu.VMEM), pl.BlockSpec(memory_space=pl.ANY)
    return pl.pallas_call(
        functools.partial(kernel, chips, nh, group, min(256, rows)),
        out_shape=jax.ShapeDtypeStruct(queries.shape, bf16),
        in_specs=[pl.BlockSpec(memory_space=pltpu.SMEM), hbm, vmem, vmem, hbm, hbm],
        out_specs=vmem,
        scratch_shapes=[
            pltpu.VMEM((slots * nh, hd), bf16),
            pltpu.VMEM((slots * nh, hd), bf16),
            pltpu.VMEM((2, CHUNK * nh, hd), f32),
            pltpu.VMEM((nh, slots + ext, 2 * hd), bf16),
            pltpu.VMEM((nh, slots + ext, 2 * hd), bf16),
            pltpu.VMEM((rows, ext), jnp.int32),
            pltpu.VMEM(queries.shape, bf16),
            pltpu.VMEM(queries.shape, bf16),
            pltpu.VMEM((far,) + queries.shape, bf16),
            pltpu.VMEM((far,) + queries.shape, bf16),
            pltpu.VMEM((nh, rows, hd), f32),
            pltpu.VMEM((nh, rows, hd), f32),
            pltpu.VMEM((nh, rows, hd), f32),
            pltpu.VMEM((nh, rows, hd), f32),
            pltpu.VMEM((nh, rows, hd), bf16),
            pltpu.VMEM((nh, lr, 128), f32),
            pltpu.VMEM((far, nh, rows, hd), bf16),
            pltpu.VMEM((far, nh, lr, 128), f32),
            pltpu.VMEM((far, nh, rows, hd), bf16),
            pltpu.VMEM((far, nh, lr, 128), f32),
            pltpu.VMEM((nh, rows, hd), bf16),
            pltpu.VMEM((nh, lr, 128), f32),
            pltpu.VMEM((far, nh, rows, hd), bf16),
            pltpu.VMEM((far, nh, lr, 128), f32),
            pltpu.VMEM((far, nh, rows, hd), bf16),
            pltpu.VMEM((far, nh, lr, 128), f32),
            pltpu.SemaphoreType.DMA((3,)),
            pltpu.SemaphoreType.DMA((n_copies,)),
            pltpu.SemaphoreType.DMA((n_copies,)),
        ],
        compiler_params=pltpu.CompilerParams(
            collective_id=0, has_side_effects=True, vmem_limit_bytes=60 * 1024 * 1024
        ),
        name="turn_attention",
    )(cache_len, queries, flat(new_keys), flat(new_values), flat(cache_keys), flat(cache_values))


def solution(mesh):
    split = P(("conv", "ctx"), "head", None)
    return jax.shard_map(
        functools.partial(per_device, mesh.shape["ctx"]),
        mesh=mesh,
        in_specs=(split, split, split, split, split, P("conv")),
        out_specs=split,
        check_vma=False,
    )
```
